128 devices in a mesh: col: 16 (over y, x_lo, core), row: 8 (over x_hi, z).
Axes of the slice: x: 4 (x_hi: 2, x_lo: 2; x = x_hi * 2 + x_lo), y: 4, z: 4, core: 2. Of those that a mesh axis runs over, the one named last changes fastest.
Arguments:
- kernel: float32 [512, 2048, 256], P('row', 'col'), may hold values from -0.0078125 to 0.0078125
- history: float32 [2048, 16, 256], P(('col', 'row')), may hold values from -6 to 6
- noise_weight: float32 [512, 256], P('row'), may hold values from 0.3 to 3
- prior_weight: float32 [2048], P(('col', 'row')), may hold values from 0.3 to 3
Outputs:
- hessian_action: float32 [2048, 16, 256], P(('col', 'row'))
The draws below stay inside these ranges and needn't reach their ends.
All inputs are finite; a program needn't handle non-finite values.
Results may differ from the reference program's by a relative error of at most 0.00005.
Values sent between devices are 32-bit elements; how exact they have to be, the bound alone decides.
No kernel may reach another device: no remote copies, remote signals or barrier semaphores. Data moves between devices by JAX's collectives and lax.ppermute only.
A program may use at most 192 MiB of HBM per device.

```python
import math
import jax
import jax.numpy as jnp

S = 512
NT = 256
R = 16
P_SIZE = 2048


def levels(own_key, dims, cuts, low, high):
    factor_of = 1.0
    for position, blocks in cuts:
        steps = jax.random.uniform(jax.random.fold_in(jax.random.fold_in(own_key, 6), position), (blocks,), jnp.float32, low / len(cuts), high / len(cuts))
        factor_of = factor_of * jnp.repeat(jnp.exp(steps), dims[position] // blocks).reshape((-1,) + (1,) * (len(dims) - 1 - position))
    return factor_of


def scatter_about(key, extent, deviation, most, pieces=(), kind=jnp.bfloat16):
    factor_of = levels(key, extent, pieces, -0.22, 0.18) if pieces else 1.0
    array = jax.random.normal(key, extent, jnp.float32) * deviation * factor_of
    return jnp.minimum(jnp.maximum(array, -most), most).astype(kind)


def setup_inputs(seed: int = 0) -> dict:
    seeds = jax.random.split(jax.random.key(seed), 5)
    kernel = scatter_about(seeds[0], (S, P_SIZE, NT), (P_SIZE * NT) ** -0.5, 0.0078125, ((0, 8), (1, 16)), jnp.float32)
    history = scatter_about(seeds[1], (P_SIZE, R, NT), 1.0, 6.0, ((0, 128),), jnp.float32)
    noise_weight = jnp.clip(jnp.exp(math.log(3.0) - 2.3025851 * jax.random.uniform(seeds[2], (S, NT), jnp.float32) ** levels(seeds[2], (S, NT), ((0, 8),), -0.2, 0.2)), 0.3, 3.0)
    prior_weight = jnp.clip(jnp.exp(math.log(3.0) - 2.3025851 * jax.random.uniform(seeds[3], (P_SIZE,), jnp.float32) ** levels(seeds[3], (P_SIZE,), ((0, 128),), -0.2, 0.2)), 0.3, 3.0)
    return dict(kernel=kernel, history=history, noise_weight=noise_weight, prior_weight=prior_weight)


def reference(kernel, history, noise_weight, prior_weight):
    steps_total = history.shape[2]
    length = 2 * steps_total
    kernel_hat = jnp.fft.rfft(kernel, n=length, axis=2)
    history_hat = jnp.fft.rfft(history, n=length, axis=2)
    data_hat = jnp.einsum('spf,prf->srf', kernel_hat, history_hat)
    data = jnp.fft.irfft(data_hat, n=length, axis=2)[:, :, :steps_total]
    weighted = data * noise_weight[:, None, :]
    weighted_hat = jnp.fft.rfft(weighted, n=length, axis=2)
    gradient_hat = jnp.einsum('spf,srf->prf', jnp.conj(kernel_hat), weighted_hat)
    gradient = jnp.fft.irfft(gradient_hat, n=length, axis=2)[:, :, :steps_total]
    result = gradient + prior_weight[:, None, None] * history
    return result.astype(jnp.float32)
```

```python
import math

import jax
import jax.numpy as jnp
import numpy as np
from jax import lax
from jax.experimental import pallas as pl
from jax.experimental.pallas import tpu as pltpu
from jax.sharding import PartitionSpec as P

bf16 = jnp.bfloat16
f32 = jnp.float32
NT = 256
NF = 256
S = 64
PL = 128
R = 16
LANE = 128


def split_np(table):
    high = table.astype(np.float32).astype(np.dtype(bf16))
    low = (table - high.astype(np.float64)).astype(np.float32).astype(np.dtype(bf16))
    return high, low


def dft_tables():
    freq = (np.arange(NF) + 0.5)[:, None]
    phase = 2.0 * math.pi * freq * np.arange(NT)[None, :] / (2 * NT)
    forward = np.concatenate([np.cos(phase), -np.sin(phase)], 0)
    inverse = forward / NF
    return split_np(forward), split_np(inverse.T.copy()), split_np(inverse)


def split(x):
    high = x.astype(bf16)
    return high, (x - high.astype(f32)).astype(bf16)


def mm(a, b, dims):
    return lax.dot_general(a, b, (dims, ((), ())), preferred_element_type=f32)


NTD = ((1,), (1,))
NND = ((1,), (0,))
TND = ((0,), (0,))


def mm3(a, b, dims):
    return mm(a[0], b[0], dims) + mm(a[0], b[1], dims) + mm(a[1], b[0], dims)


def const_spec(shape):
    return pl.BlockSpec(shape, lambda *_: (0,) * len(shape), pipeline_mode=pl.Buffered(1))


SB = 16


def kernel_dft_body(x_ref, th_ref, tl_ref, o_ref, sc_ref):
    table = (th_ref[...], tl_ref[...])
    for j in range(0, SB, 2):
        x = x_ref[j : j + 2].reshape(2 * PL, NT)
        y = mm3(table, split(x), NTD)
        sc_ref[pl.ds(j, 2 * NF, stride=SB), :] = y[:, :LANE]
        sc_ref[pl.ds(j + 1, 2 * NF, stride=SB), :] = y[:, LANE:]
    step = 16
    for c in range(2):

        def body(i, carry):
            base = pl.multiple_of(i * step, step)
            v = sc_ref[pl.ds(pl.multiple_of((c * NF + base) * SB, step * SB), step * SB), :]
            high, low = split(v)
            o_ref[pl.ds(base, step), c, 0] = high.reshape(step, SB, LANE)
            o_ref[pl.ds(base, step), c, 1] = low.reshape(step, SB, LANE)
            return carry

        lax.fori_loop(0, NF // step, body, 0)


def kernel_dft(kernel, th, tl):
    return pl.pallas_call(
        kernel_dft_body,
        grid=(S // SB,),
        in_specs=[
            pl.BlockSpec((SB, PL, NT), lambda i: (i, 0, 0)),
            const_spec((2 * NF, NT)),
            const_spec((2 * NF, NT)),
        ],
        out_specs=pl.BlockSpec((NF, 2, 2, SB, LANE), lambda i: (0, 0, 0, i, 0)),
        out_shape=jax.ShapeDtypeStruct((NF, 2, 2, S, LANE), bf16),
        scratch_shapes=[pltpu.VMEM((2 * NF * SB, LANE), f32)],
        compiler_params=pltpu.CompilerParams(vmem_limit_bytes=48 << 20),
        name="kernel_dft",
    )(kernel, th, tl)


FB = 16


def forward_body(pos_ref, k_ref, th_ref, tl_ref, ih_ref, il_ref, *refs):
    chunks = refs[:8]
    o_ref, hist_ref, h_ref, d_ref, sem = refs[8:]
    step = pl.program_id(0)

    @pl.when(step == 0)
    def _():
        copies = [
            pltpu.make_async_copy(chunks[d], hist_ref.at[pos_ref[d]], sem.at[d]) for d in range(8)
        ]
        for c in copies:
            c.start()
        for c in copies:
            c.wait()
        table = (th_ref[...], tl_ref[...])
        for r in range(R):
            x = hist_ref[:, :, r].reshape(PL, NT)
            y = mm3(table, split(x), NTD)
            h_ref[pl.ds(r, 2 * NF, stride=R), :] = y

    def body(i, carry):
        f = step * FB + i
        base = pl.multiple_of(f * R, R)
        re = split(h_ref[pl.ds(base, R), :])
        im = split(h_ref[pl.ds(pl.multiple_of(NF * R + base, R), R), :])
        lhs = jnp.concatenate(
            [
                jnp.concatenate([re[0], -im[0]], 1),
                jnp.concatenate([im[0], re[0]], 1),
                jnp.concatenate([re[1], -im[1]], 1),
                jnp.concatenate([im[1], re[1]], 1),
            ],
            0,
        )
        k_re = k_ref[i, 0].reshape(2 * S, LANE)
        k_im = k_ref[i, 1].reshape(2 * S, LANE)
        out = mm(lhs, jnp.concatenate([k_re, k_im], 1), NTD)
        out = out[: 2 * R] + out[2 * R :]
        d_ref[pl.ds(pl.multiple_of(f * 2 * R, 2 * R), 2 * R), :] = out
        return carry

    lax.fori_loop(0, FB, body, 0, unroll=4)

    @pl.when(step == pl.num_programs(0) - 1)
    def _():
        table = (ih_ref[...], il_ref[...])
        lane = lax.broadcasted_iota(jnp.int32, (NT, LANE), 1)
        for r in range(0, R, 2):
            halves = []
            for q in (r, r + 1):
                re = d_ref[pl.ds(q, NF, stride=2 * R), :]
                im = d_ref[pl.ds(R + q, NF, stride=2 * R), :]
                y = mm3(table, split(jnp.concatenate([re, im], 0)), NND)
                halves.append(y + pltpu.roll(y, S, 1))
            o_ref[:, (r // 2) * LANE : (r // 2 + 1) * LANE] = jnp.where(lane < S, halves[0], halves[1])


def forward(pos, k_hat, tables, chunks):
    (th, tl), (ih, il), _ = tables
    grid_spec = pltpu.PrefetchScalarGridSpec(
        num_scalar_prefetch=1,
        grid=(NF // FB,),
        in_specs=[
            pl.BlockSpec((FB, 2, 2, S, LANE), lambda i, p: (i, 0, 0, 0, 0)),
            const_spec((2 * NF, NT)),
            const_spec((2 * NF, NT)),
            const_spec((NT, 2 * NF)),
            const_spec((NT, 2 * NF)),
        ]
        + [pl.BlockSpec(memory_space=pl.ANY)] * 8,
        out_specs=pl.BlockSpec((NT, R * S), lambda i, p: (0, 0), pipeline_mode=pl.Buffered(1)),
        scratch_shapes=[
            pltpu.VMEM((8, R, R, NT), f32),
            pltpu.VMEM((2 * NF * R, LANE), f32),
            pltpu.VMEM((2 * NF * R, LANE), f32),
            pltpu.SemaphoreType.DMA((8,)),
        ],
    )
    return pl.pallas_call(
        forward_body,
        grid_spec=grid_spec,
        out_shape=jax.ShapeDtypeStruct((NT, R * S), f32),
        compiler_params=pltpu.CompilerParams(vmem_limit_bytes=48 << 20),
        name="forward",
    )(pos, k_hat, th, tl, ih, il, *chunks)


def adjoint_body(core_ref, k_ref, th_ref, tl_ref, ih_ref, il_ref, nw_ref, own_ref, other_ref, o_ref, w_ref, g_ref, wt_ref):
    step = pl.program_id(0)
    half = NT // 2

    @pl.when(step == 0)
    def _():
        core = core_ref[0]
        wt_ref[pl.ds(pl.multiple_of(core * half, half), half), :] = own_ref[...]
        wt_ref[pl.ds(pl.multiple_of((1 - core) * half, half), half), :] = other_ref[...]
        table = (th_ref[...], tl_ref[...])
        nw = nw_ref[...]
        low_t = lax.broadcasted_iota(jnp.int32, (NT, LANE), 1) < S
        low_f = lax.broadcasted_iota(jnp.int32, (NF, LANE), 1) < S
        for j in range(R // 2):
            a = wt_ref[:, j * LANE : (j + 1) * LANE] * nw
            b = pltpu.roll(a, S, 1)
            for q, x in ((2 * j, jnp.where(low_t, a, b)), (2 * j + 1, jnp.where(low_t, b, a))):
                y = mm3(table, split(x), NND)
                re, im = y[:NF], y[NF:]
                w_ref[pl.ds(q, NF, stride=2 * R), :] = jnp.where(low_f, re, im)
                w_ref[pl.ds(R + q, NF, stride=2 * R), :] = jnp.where(low_f, im, -re)

    def body(i, carry):
        base = pl.multiple_of((step * FB + i) * 2 * R, 2 * R)
        high, low = split(w_ref[pl.ds(base, 2 * R), :])
        lhs = jnp.concatenate([high, low], 0)
        rhs = jnp.concatenate(
            [
                jnp.concatenate([k_ref[i, 0, 0], k_ref[i, 0, 1]], 1),
                jnp.concatenate([k_ref[i, 1, 0], k_ref[i, 1, 1]], 1),
            ],
            0,
        )
        out = mm(lhs, rhs, NND)
        out = out[: 2 * R] + out[2 * R :]
        g_ref[pl.ds(base, 2 * R), :] = out[:, :LANE] + out[:, LANE:]
        return carry

    lax.fori_loop(0, FB, body, 0, unroll=4)

    @pl.when(step == pl.num_programs(0) - 1)
    def _():
        table = (ih_ref[...], il_ref[...])
        for r in range(R):
            re = g_ref[pl.ds(r, NF, stride=2 * R), :]
            im = g_ref[pl.ds(R + r, NF, stride=2 * R), :]
            y = mm3(split(jnp.concatenate([re, im], 0)), table, TND)
            o_ref[:, r] = y.reshape(8, R, NT)


def adjoint(core, k_hat, tables, noise, own, other):
    (th, tl), _, (ih, il) = tables
    grid_spec = pltpu.PrefetchScalarGridSpec(
        num_scalar_prefetch=1,
        grid=(NF // FB,),
        in_specs=[
            pl.BlockSpec((FB, 2, 2, S, LANE), lambda i, p: (i, 0, 0, 0, 0)),
            const_spec((2 * NF, NT)),
            const_spec((2 * NF, NT)),
            const_spec((2 * NF, NT)),
            const_spec((2 * NF, NT)),
            const_spec((NT, LANE)),
            const_spec((NT // 2, R * S)),
            const_spec((NT // 2, R * S)),
        ],
        out_specs=pl.BlockSpec((8, R, R, NT), lambda i, p: (0, 0, 0, 0), pipeline_mode=pl.Buffered(1)),
        scratch_shapes=[
            pltpu.VMEM((2 * NF * R, LANE), f32),
            pltpu.VMEM((2 * NF * R, LANE), f32),
            pltpu.VMEM((NT, R * S), f32),
        ],
    )
    return pl.pallas_call(
        adjoint_body,
        grid_spec=grid_spec,
        out_shape=jax.ShapeDtypeStruct((8, R, R, NT), f32),
        compiler_params=pltpu.CompilerParams(vmem_limit_bytes=48 << 20),
        name="adjoint",
    )(core, k_hat, th, tl, ih, il, noise, own, other)


def row_perm(d):
    return [(i, ((i & 4) ^ (d & 4)) | ((i + d) & 3)) for i in range(8)]


CORE_SWAP = [(i, i ^ 1) for i in range(16)]
CHIP_GROUPS = [list(range(0, 16, 2)), list(range(1, 16, 2))]


def local(kernel, history, noise_weight, prior_weight):
    tables = dft_tables()
    row = lax.axis_index("row")
    col = lax.axis_index("col")
    core = col & 1

    chunks = [history] + [lax.ppermute(history, "row", row_perm(d)) for d in range(1, 8)]
    pos = jnp.stack([((row & 4) ^ (d & 4)) | ((row - d) & 3) for d in range(8)]).astype(jnp.int32)
    noise = jnp.concatenate([noise_weight.T, noise_weight.T], 1)

    k_hat = kernel_dft(kernel, *tables[0])
    data = forward(pos, k_hat, tables, chunks)

    half = NT // 2
    mine = lax.dynamic_slice(data, (core * half, 0), (half, R * S))
    theirs = lax.dynamic_slice(data, ((1 - core) * half, 0), (half, R * S))
    mine = mine + lax.ppermute(theirs, "col", CORE_SWAP)
    parts = lax.all_to_all(
        mine.reshape(8, half // 8, R * S), "col", 0, 0, axis_index_groups=CHIP_GROUPS, tiled=True
    )
    total = parts.sum(0)
    spread = jnp.broadcast_to(total, (8, half // 8, R * S))
    own = lax.all_to_all(spread, "col", 0, 0, axis_index_groups=CHIP_GROUPS, tiled=True).reshape(half, R * S)
    other = lax.ppermute(own, "col", CORE_SWAP)

    grad = adjoint(core.reshape(1).astype(jnp.int32), k_hat, tables, noise, own, other)
    grad = lax.all_to_all(grad, "row", 0, 0, tiled=True).sum(0)
    return jnp.swapaxes(grad, 0, 1) + prior_weight[:, None, None] * history


def solution(mesh):
    in_specs = (
        P("row", "col", None),
        P(("col", "row"), None, None),
        P("row", None),
        P(("col", "row")),
    )
    out_specs = P(("col", "row"), None, None)
    return jax.shard_map(local, mesh=mesh, in_specs=in_specs, out_specs=out_specs, check_vma=False)
```

```python
import math

import jax
import jax.numpy as jnp
import numpy as np
from jax import lax
from jax.experimental import pallas as pl
from jax.experimental.pallas import tpu as pltpu
from jax.sharding import PartitionSpec as P

bf16 = jnp.bfloat16
f32 = jnp.float32
NT = 256
NF = 256
S = 64
PL = 128
R = 16
LANE = 128


def split_np(table):
    high = table.astype(np.float32).astype(np.dtype(bf16))
    low = (table - high.astype(np.float64)).astype(np.float32).astype(np.dtype(bf16))
    return high, low


def dft_tables():
    freq = (np.arange(NF) + 0.5)[:, None]
    phase = 2.0 * math.pi * freq * np.arange(NT)[None, :] / (2 * NT)
    forward = np.concatenate([np.cos(phase), -np.sin(phase)], 0)
    inverse = forward / NF
    return split_np(forward), split_np(inverse.T.copy()), split_np(inverse)


def split(x):
    high = x.astype(bf16)
    return high, (x - high.astype(f32)).astype(bf16)


def in_hbm(arrays):
    return [pltpu.with_memory_space_constraint(jnp.asarray(x), pltpu.HBM) for x in arrays]


def mm(a, b, dims):
    return lax.dot_general(a, b, (dims, ((), ())), preferred_element_type=f32)


NTD = ((1,), (1,))
NND = ((1,), (0,))
TND = ((0,), (0,))


def mm3(a, b, dims):
    return mm(a[0], b[0], dims) + mm(a[0], b[1], dims) + mm(a[1], b[0], dims)


def const_spec(shape):
    return pl.BlockSpec(shape, lambda *_: (0,) * len(shape), pipeline_mode=pl.Buffered(1))


SB = 16
G8 = 8


def kernel_dft_body(x_ref, th_ref, tl_ref, o_ref, sc_ref):
    table = (th_ref[...], tl_ref[...])
    for j in range(0, SB, 2):
        x = x_ref[j : j + 2].reshape(2 * PL, NT)
        y = mm3(table, split(x), NTD)
        for q in (j, j + 1):
            group = q // G8 * 2 * NF * G8
            sc_ref[pl.ds(group + q % G8, 2 * NF, stride=G8), :] = y[:, (q - j) * LANE : (q - j + 1) * LANE]
    step = 16
    for c in range(2):

        def body(i, carry):
            base = pl.multiple_of(i * step, step)
            v = jnp.concatenate(
                [
                    sc_ref[
                        pl.ds(pl.multiple_of(((g * 2 + c) * NF + base) * G8, step * G8), step * G8), :
                    ].reshape(step, G8, LANE)
                    for g in range(SB // G8)
                ],
                1,
            )
            high, low = split(v)
            o_ref[pl.ds(base, step), c, 0] = high
            o_ref[pl.ds(base, step), c, 1] = low
            return carry

        lax.fori_loop(0, NF // step, body, 0)


def kernel_dft(kernel, th, tl):
    return pl.pallas_call(
        kernel_dft_body,
        grid=(S // SB,),
        in_specs=[
            pl.BlockSpec((SB, PL, NT), lambda i: (i, 0, 0)),
            const_spec((2 * NF, NT)),
            const_spec((2 * NF, NT)),
        ],
        out_specs=pl.BlockSpec((NF, 2, 2, SB, LANE), lambda i: (0, 0, 0, i, 0)),
        out_shape=pltpu.HBM((NF, 2, 2, S, LANE), bf16),
        scratch_shapes=[pltpu.VMEM((2 * NF * SB, LANE), f32)],
        compiler_params=pltpu.CompilerParams(vmem_limit_bytes=24 << 20),
        name="kernel_dft",
    )(*in_hbm([kernel, th, tl]))


def put_rows(ref, part, q, value):
    group = (part * (R // G8) + q // G8) * NF * G8
    ref[pl.ds(group + q % G8, NF, stride=G8), :] = value


def get_rows(ref, part, q):
    group = (part * (R // G8) + q // G8) * NF * G8
    return ref[pl.ds(group + q % G8, NF, stride=G8), :]


def freq_at(part, g, f):
    return pl.ds(pl.multiple_of(((part * (R // G8) + g) * NF + f) * G8, G8), G8)


def get_freq(ref, part, f):
    return jnp.concatenate([ref[freq_at(part, g, f), :] for g in range(R // G8)], 0)


def put_freq(ref, f, value):
    for part in range(2):
        for g in range(R // G8):
            at = part * R + g * G8
            ref[freq_at(part, g, f), :] = value[at : at + G8]


AHEAD = 3
KB = 8
FB = NF // KB


def fetch_blocks(k_hbm, k_ref, sem):
    return [
        pltpu.make_async_copy(k_hbm.at[pl.ds(b * FB, FB)], k_ref.at[pl.ds(b * FB, FB)], sem.at[b])
        for b in range(KB)
    ]


def fetch_tables(tables, t_ref, sem):
    copies = [pltpu.make_async_copy(table, t_ref.at[n], sem.at[n]) for n, table in enumerate(tables)]
    for c in copies:
        c.start()
    return copies


def for_each_frequency(copies, body):
    for b in range(KB):
        copies[b].wait()
        if b + AHEAD < KB:
            copies[b + AHEAD].start()
        lax.fori_loop(b * FB // 2, (b + 1) * FB // 2, body, 0, unroll=16)


def forward_body(row_ref, k_hbm, th_ref, tl_ref, ih_ref, il_ref, *refs):
    chunks = refs[:8]
    o_ref, k_ref, t_ref, i_ref, hist_ref, h_ref, d_ref, sem, t_sem, i_sem = refs[8:]
    t_copies = fetch_tables((th_ref, tl_ref), t_ref, t_sem)
    copies = fetch_blocks(k_hbm, k_ref, sem)
    row = row_ref[0]
    for d in range(8):
        hist_ref[((row & 4) ^ (d & 4)) | ((row - d) & 3)] = chunks[d][...]
    for c in t_copies:
        c.wait()
    copies[0].start()
    copies[1].start()
    i_copies = fetch_tables((ih_ref, il_ref), i_ref, i_sem)
    table = (t_ref[0], t_ref[1])
    for r in range(0, R, 2):
        x = jnp.concatenate([hist_ref[:, q].reshape(PL, NT) for q in (r, r + 1)], 0)
        y = mm3(table, split(x), NTD)
        for q in (r, r + 1):
            for part in range(2):
                put_rows(h_ref, part, q, y[part * NF : (part + 1) * NF, (q - r) * LANE : (q - r + 1) * LANE])
        if r in (6,):
            copies[2].start()

    def body(pair, carry):
        lhs, rhs = [], []
        for f in (2 * pair, 2 * pair + 1):
            re = split(get_freq(h_ref, 0, f))
            im = split(get_freq(h_ref, 1, f))
            for n in range(2):
                lhs.append(jnp.concatenate([re[n], -im[n]], 1))
                lhs.append(jnp.concatenate([im[n], re[n]], 1))
            rhs.append(jnp.concatenate([k_ref[f, c].reshape(2 * S, LANE) for c in range(2)], 1))
        out = mm(jnp.concatenate(lhs, 0), jnp.concatenate(rhs, 0), NTD)
        for n in range(2):
            own = out[4 * R * n : 4 * R * (n + 1), LANE * n : LANE * (n + 1)]
            put_freq(d_ref, 2 * pair + n, own[: 2 * R] + own[2 * R :])
        return carry

    for_each_frequency(copies, body)

    for c in i_copies:
        c.wait()
    table = (i_ref[0], i_ref[1])
    lane = lax.broadcasted_iota(jnp.int32, (NT, LANE), 1)
    for r in range(0, R, 2):
        spec = jnp.concatenate(
            [jnp.concatenate([get_rows(d_ref, part, q) for q in (r, r + 1)], 1) for part in range(2)], 0
        )
        y = mm3(table, split(spec), NND)
        halves = [y[:, :LANE] + pltpu.roll(y[:, :LANE], S, 1), y[:, LANE:] + pltpu.roll(y[:, LANE:], S, 1)]
        o_ref[:, (r // 2) * LANE : (r // 2 + 1) * LANE] = jnp.where(lane < S, halves[0], halves[1])


VMEM_SPEC = pl.BlockSpec(memory_space=pltpu.VMEM)
HBM_SPEC = pl.BlockSpec(memory_space=pl.ANY)
SMEM_SPEC = pl.BlockSpec(memory_space=pltpu.SMEM)
SPEC_ROWS = pltpu.VMEM((2 * NF * R, LANE), f32)
K_SCRATCH = pltpu.VMEM((NF, 2, 2, S, LANE), bf16)


def forward(row, k_hat, tables, chunks):
    (th, tl), (ih, il), _ = tables
    return pl.pallas_call(
        forward_body,
        in_specs=[SMEM_SPEC] + [HBM_SPEC] * 5 + [VMEM_SPEC] * 8,
        out_specs=VMEM_SPEC,
        scratch_shapes=[
            K_SCRATCH,
            pltpu.VMEM((2, 2 * NF, NT), bf16),
            pltpu.VMEM((2, NT, 2 * NF), bf16),
            pltpu.VMEM((8, R, R, NT), f32),
            SPEC_ROWS,
            SPEC_ROWS,
            pltpu.SemaphoreType.DMA((KB,)),
            pltpu.SemaphoreType.DMA((2,)),
            pltpu.SemaphoreType.DMA((2,)),
        ],
        out_shape=jax.ShapeDtypeStruct((NT, R * S), f32),
        compiler_params=pltpu.CompilerParams(vmem_limit_bytes=36 << 20),
        name="forward",
    )(row, *in_hbm([k_hat, th, tl, ih, il]), *chunks)


def adjoint_body(core_ref, k_hbm, th_ref, tl_ref, ih_ref, il_ref, *refs):
    nw_ref, own_ref, other_ref, o_ref, k_ref, t_ref, i_ref, w_ref, g_ref, wt_ref, sem, t_sem, i_sem = refs
    t_copies = fetch_tables((th_ref, tl_ref), t_ref, t_sem)
    copies = fetch_blocks(k_hbm, k_ref, sem)
    half = NT // 2
    core = core_ref[0]
    wt_ref[pl.ds(pl.multiple_of(core * half, half), half), :] = own_ref[...]
    wt_ref[pl.ds(pl.multiple_of((1 - core) * half, half), half), :] = other_ref[...]
    for c in t_copies:
        c.wait()
    copies[0].start()
    copies[1].start()
    i_copies = fetch_tables((ih_ref, il_ref), i_ref, i_sem)
    table = (t_ref[0], t_ref[1])
    nw = nw_ref[...]
    low_t = lax.broadcasted_iota(jnp.int32, (NT, LANE), 1) < S
    low_f = lax.broadcasted_iota(jnp.int32, (NF, LANE), 1) < S
    for j in range(R // 2):
        a = wt_ref[:, j * LANE : (j + 1) * LANE] * nw
        b = pltpu.roll(a, S, 1)
        x = jnp.concatenate([jnp.where(low_t, a, b), jnp.where(low_t, b, a)], 1)
        y = mm3(table, split(x), NND)
        for n in range(2):
            re = y[:NF, n * LANE : (n + 1) * LANE]
            im = y[NF:, n * LANE : (n + 1) * LANE]
            put_rows(w_ref, 0, 2 * j + n, jnp.where(low_f, re, im))
            put_rows(w_ref, 1, 2 * j + n, jnp.where(low_f, im, -re))
        if j in (3,):
            copies[2].start()

    def body(pair, carry):
        zero = jnp.zeros((4 * R, LANE), bf16)
        lhs, rhs = [], []
        for n in range(2):
            f = 2 * pair + n
            parts = split(jnp.concatenate([get_freq(w_ref, part, f) for part in range(2)], 0))
            own = jnp.concatenate(parts, 0)
            lhs.append(jnp.concatenate([own, zero] if n == 0 else [zero, own], 1))
            for c in range(2):
                rhs.append(jnp.concatenate([k_ref[f, c, 0], k_ref[f, c, 1]], 1))
        out = mm(jnp.concatenate(lhs, 0), jnp.concatenate(rhs, 0), NND)
        for n in range(2):
            own = out[4 * R * n : 4 * R * (n + 1)]
            own = own[: 2 * R] + own[2 * R :]
            put_freq(g_ref, 2 * pair + n, own[:, :LANE] + own[:, LANE:])
        return carry

    for_each_frequency(copies, body)

    for c in i_copies:
        c.wait()
    table = (i_ref[0], i_ref[1])
    for r in range(R):
        spec = jnp.concatenate([get_rows(g_ref, part, r) for part in range(2)], 0)
        y = mm3(split(spec), table, TND)
        o_ref[:, r] = y.reshape(8, R, NT)


def adjoint(core, k_hat, tables, noise, own, other):
    (th, tl), _, (ih, il) = tables
    return pl.pallas_call(
        adjoint_body,
        in_specs=[SMEM_SPEC] + [HBM_SPEC] * 5 + [VMEM_SPEC] * 3,
        out_specs=VMEM_SPEC,
        scratch_shapes=[
            K_SCRATCH,
            pltpu.VMEM((2, 2 * NF, NT), bf16),
            pltpu.VMEM((2, 2 * NF, NT), bf16),
            SPEC_ROWS,
            SPEC_ROWS,
            pltpu.VMEM((NT, R * S), f32),
            pltpu.SemaphoreType.DMA((KB,)),
            pltpu.SemaphoreType.DMA((2,)),
            pltpu.SemaphoreType.DMA((2,)),
        ],
        out_shape=jax.ShapeDtypeStruct((8, R, R, NT), f32),
        compiler_params=pltpu.CompilerParams(vmem_limit_bytes=36 << 20),
        name="adjoint",
    )(core, *in_hbm([k_hat, th, tl, ih, il]), noise, own, other)


def row_perm(d):
    return [(i, ((i & 4) ^ (d & 4)) | ((i + d) & 3)) for i in range(8)]


CORE_SWAP = [(i, i ^ 1) for i in range(16)]
CHIP_GROUPS = [list(range(0, 16, 2)), list(range(1, 16, 2))]


def local(kernel, history, noise_weight, prior_weight):
    tables = dft_tables()
    row = lax.axis_index("row")
    col = lax.axis_index("col")
    core = col & 1

    by_vector = jnp.swapaxes(history, 0, 1)
    chunks = [by_vector] + [lax.ppermute(by_vector, "row", row_perm(d)) for d in range(1, 8)]
    noise = jnp.concatenate([noise_weight.T, noise_weight.T], 1)

    k_hat = kernel_dft(kernel, *tables[0])
    data = forward(row.reshape(1).astype(jnp.int32), k_hat, tables, chunks)

    half = NT // 2
    mine = lax.dynamic_slice(data, (core * half, 0), (half, R * S))
    theirs = lax.dynamic_slice(data, ((1 - core) * half, 0), (half, R * S))
    mine = mine + lax.ppermute(theirs, "col", CORE_SWAP)
    parts = lax.all_to_all(
        mine.reshape(8, half // 8, R * S), "col", 0, 0, axis_index_groups=CHIP_GROUPS, tiled=True
    )
    total = parts.sum(0)
    spread = jnp.broadcast_to(total, (8, half // 8, R * S))
    own = lax.all_to_all(spread, "col", 0, 0, axis_index_groups=CHIP_GROUPS, tiled=True).reshape(half, R * S)
    other = lax.ppermute(own, "col", CORE_SWAP)

    grad = adjoint(core.reshape(1).astype(jnp.int32), k_hat, tables, noise, own, other)
    grad = lax.all_to_all(grad, "row", 0, 0, tiled=True).sum(0)
    return jnp.swapaxes(grad, 0, 1) + prior_weight[:, None, None] * history


def solution(mesh):
    in_specs = (
        P("row", "col", None),
        P(("col", "row"), None, None),
        P("row", None),
        P(("col", "row")),
    )
    out_specs = P(("col", "row"), None, None)
    return jax.shard_map(local, mesh=mesh, in_specs=in_specs, out_specs=out_specs, check_vma=False)
```

```python
import math

import jax
import jax.numpy as jnp
import numpy as np
from jax import lax
from jax.experimental import pallas as pl
from jax.experimental.pallas import tpu as pltpu
from jax.sharding import PartitionSpec as P

bf16 = jnp.bfloat16
f32 = jnp.float32
NT = 256
NF = 256
S = 64
PL = 128
R = 16
LANE = 128


def split_np(table):
    high = table.astype(np.float32).astype(np.dtype(bf16))
    low = (table - high.astype(np.float64)).astype(np.float32).astype(np.dtype(bf16))
    return high, low


def dft_tables():
    omega = 2.0 * math.pi * (np.arange(NF) + 0.5)[:, None] / (2 * NT)
    phase = omega * ((NT - 1) / 2 - np.arange(NT // 2))[None, :]
    folded = []
    for table in (np.cos(phase), np.sin(phase)):
        high, low = split_np(table)
        rows = np.concatenate([high, low], 0)
        folded.append(np.concatenate([rows, rows], 1))
    after = omega * (FOLD_ORDER - (NT - 1))[None, :]
    inverse = np.concatenate([np.cos(after), -np.sin(after)], 0) / NF
    after = omega * np.arange(NT)[None, :]
    adjoint_inverse = np.concatenate([np.cos(after), -np.sin(after)], 0) / NF
    return folded, split_np(inverse.T.copy()), split_np(adjoint_inverse)


def split(x):
    high = x.astype(bf16)
    return high, (x - high.astype(f32)).astype(bf16)


def in_hbm(arrays):
    return [pltpu.with_memory_space_constraint(jnp.asarray(x), pltpu.HBM) for x in arrays]


def mm(a, b, dims):
    return lax.dot_general(a, b, (dims, ((), ())), preferred_element_type=f32)


NTD = ((1,), (1,))
NND = ((1,), (0,))
TND = ((0,), (0,))


def mm3(a, b, dims):
    return mm(a[0], b[0], dims) + mm(a[0], b[1], dims) + mm(a[1], b[0], dims)


def transform(tables, first, mirrored, axis):
    parts = []
    for table, folded in zip(tables, (first + mirrored, first - mirrored)):
        y = mm(table, jnp.concatenate(split(folded), axis), NTD if axis else NND)
        parts.append(y[:NF] + y[NF:])
    return parts


def transform_rows(tables, x):
    half = NT // 2
    back = half - 1 - lax.broadcasted_iota(jnp.int32, (x.shape[0], half), 1)
    return transform(tables, x[:, :half], jnp.take_along_axis(x[:, half:], back, axis=1), 1)


def const_spec(shape):
    return pl.BlockSpec(shape, lambda *_: (0,) * len(shape), pipeline_mode=pl.Buffered(1))


SB = 16
FOLD_ORDER = np.concatenate([np.arange(NT // 2), np.arange(NT - 1, NT // 2 - 1, -1)])
G8 = 8


def kernel_dft_body(x_ref, th_ref, tl_ref, o_ref, sc_ref):
    table = (th_ref[...], tl_ref[...])
    for j in range(0, SB, 2):
        x = x_ref[j : j + 2].reshape(2 * PL, NT)
        for part, y in enumerate(transform_rows(table, x)):
            for q in (j, j + 1):
                group = (q // G8 * 2 + part) * NF * G8
                sc_ref[pl.ds(group + q % G8, NF, stride=G8), :] = y[:, (q - j) * LANE : (q - j + 1) * LANE]
    step = 16
    for c in range(2):

        def body(i, carry):
            base = pl.multiple_of(i * step, step)
            v = jnp.concatenate(
                [
                    sc_ref[
                        pl.ds(pl.multiple_of(((g * 2 + c) * NF + base) * G8, step * G8), step * G8), :
                    ].reshape(step, G8, LANE)
                    for g in range(SB // G8)
                ],
                1,
            )
            high, low = split(v)
            rows = pl.ds(pl.multiple_of(pl.program_id(0) * SB, SB), SB)
            o_ref[pl.ds(base, step), c, 0, rows] = high
            o_ref[pl.ds(base, step), c, 1, rows] = low
            return carry

        lax.fori_loop(0, NF // step, body, 0)


def in_vmem(x):
    return pltpu.with_memory_space_constraint(x, pltpu.VMEM)


def kernel_dft(kernel, tables, first, steps):
    return pl.pallas_call(
        kernel_dft_body,
        grid=(steps,),
        in_specs=[
            pl.BlockSpec((SB, PL, NT), lambda i: (i + first, 0, 0)),
            const_spec((2 * NF, NT)),
            const_spec((2 * NF, NT)),
        ],
        out_specs=pl.BlockSpec(memory_space=pltpu.VMEM),
        out_shape=pltpu.VMEM((NF, 2, 2, steps * SB, LANE), bf16),
        scratch_shapes=[pltpu.VMEM((2 * NF * SB, LANE), f32)],
        compiler_params=pltpu.CompilerParams(vmem_limit_bytes=16 << 20),
        name="kernel_dft",
    )(*in_hbm([kernel, *tables]))


def put_rows(ref, part, q, value):
    group = (part * (R // G8) + q // G8) * NF * G8
    ref[pl.ds(group + q % G8, NF, stride=G8), :] = value


def get_rows(ref, part, q):
    group = (part * (R // G8) + q // G8) * NF * G8
    return ref[pl.ds(group + q % G8, NF, stride=G8), :]


def freq_at(part, g, f):
    return pl.ds(pl.multiple_of(((part * (R // G8) + g) * NF + f) * G8, G8), G8)


def get_freq(ref, part, f):
    return jnp.concatenate([ref[freq_at(part, g, f), :] for g in range(R // G8)], 0)


def put_freq(ref, f, value):
    for part in range(2):
        for g in range(R // G8):
            at = part * R + g * G8
            ref[freq_at(part, g, f), :] = value[at : at + G8]


AHEAD = 3
KB = 8
FB = NF // KB


def fetch_blocks(k_hbm, k_ref, sem):
    return [
        [pltpu.make_async_copy(k_hbm.at[pl.ds(b * FB, FB)], k_ref.at[pl.ds(b * FB, FB)], sem.at[b])]
        for b in range(KB)
    ]


def start(copies):
    for c in copies:
        c.start()


def wait(copies):
    for c in copies:
        c.wait()


def fetch_tables(tables, t_ref, sem):
    copies = [pltpu.make_async_copy(table, t_ref.at[n], sem.at[n]) for n, table in enumerate(tables)]
    for c in copies:
        c.start()
    return copies


def for_each_frequency(copies, body):
    for b in range(KB):
        wait(copies[b])
        if b + AHEAD < KB:
            start(copies[b + AHEAD])
        lax.fori_loop(b * FB // 2, (b + 1) * FB // 2, body, 0, unroll=16)


def forward_body(row_ref, k1_hbm, k2_ref, th_ref, tl_ref, ih_ref, il_ref, *refs):
    own, across, *own_z = refs[:5]
    along, both = refs[5:7]
    o_ref, k_hbm, k1_ref, t_ref, i_ref, hist_ref, h_ref, d_ref, sem, t_sem, i_sem = refs[7:]
    t_copies = fetch_tables((th_ref, tl_ref), t_ref, t_sem)
    k1_copy = pltpu.make_async_copy(k1_hbm, k1_ref, sem.at[0])
    k1_out = pltpu.make_async_copy(k1_ref, k_hbm.at[:, :, :, pl.ds(0, SB)], sem.at[1])
    k2_out = pltpu.make_async_copy(k2_ref, k_hbm.at[:, :, :, pl.ds(SB, S - SB)], sem.at[2])
    hi, z = row_ref[0] >> 2, row_ref[0] & 3
    for n, d in enumerate((0,) + Z_STEPS):
        for m in range(2):
            at = (hi if m == 0 else 1 - hi) * 4 + ((z - d) & 3)
            first = (own, across)[m][...] if n == 0 else own_z[n - 1][m]
            hist_ref[at, : R // 2] = first
            hist_ref[at, R // 2 :] = (along, both)[m][n]
    for c in t_copies:
        c.wait()
    k1_copy.start()
    i_copies = fetch_tables((ih_ref, il_ref), i_ref, i_sem)
    table = (t_ref[0], t_ref[1])
    for r in range(0, R, 2):
        x = jnp.concatenate([hist_ref[:, q].reshape(PL, NT) for q in (r, r + 1)], 0)
        for part, y in enumerate(transform_rows(table, x)):
            for q in (r, r + 1):
                put_rows(h_ref, part, q, y[:, (q - r) * LANE : (q - r + 1) * LANE])

    def body(pair, carry):
        lhs, rhs = [], []
        for f in (2 * pair, 2 * pair + 1):
            re = split(get_freq(h_ref, 0, f))
            im = split(get_freq(h_ref, 1, f))
            for n in range(2):
                lhs.append(jnp.concatenate([re[n], -im[n]], 1))
                lhs.append(jnp.concatenate([im[n], re[n]], 1))
            rhs.append(
                jnp.concatenate(
                    [
                        jnp.concatenate([k[f, c, n] for n in range(2) for k in (k1_ref, k2_ref)], 0)
                        for c in range(2)
                    ],
                    1,
                )
            )
        out = mm(jnp.concatenate(lhs, 0), jnp.concatenate(rhs, 0), NTD)
        for n in range(2):
            own = out[4 * R * n : 4 * R * (n + 1), LANE * n : LANE * (n + 1)]
            put_freq(d_ref, 2 * pair + n, own[: 2 * R] + own[2 * R :])
        return carry

    k1_copy.wait()
    k1_out.start()
    k2_out.start()
    lax.fori_loop(0, NF // 2, body, 0, unroll=16)

    for c in i_copies:
        c.wait()
    table = (i_ref[0], i_ref[1])
    lane = lax.broadcasted_iota(jnp.int32, (NT, LANE), 1)
    for r in range(0, R, 2):
        spec = jnp.concatenate(
            [jnp.concatenate([get_rows(d_ref, part, q) for q in (r, r + 1)], 1) for part in range(2)], 0
        )
        y = mm3(table, split(spec), NND)
        halves = [y[:, :LANE] + pltpu.roll(y[:, :LANE], S, 1), y[:, LANE:] + pltpu.roll(y[:, LANE:], S, 1)]
        o_ref[:, (r // 2) * LANE : (r // 2 + 1) * LANE] = jnp.where(lane < S, halves[0], halves[1])
    k1_out.wait()
    k2_out.wait()


VMEM_SPEC = pl.BlockSpec(memory_space=pltpu.VMEM)
HBM_SPEC = pl.BlockSpec(memory_space=pl.ANY)
SMEM_SPEC = pl.BlockSpec(memory_space=pltpu.SMEM)
SPEC_ROWS = pltpu.VMEM((2 * NF * R, LANE), f32)
K_SCRATCH = pltpu.VMEM((NF, 2, 2, S, LANE), bf16)


def forward(row, k1, k2, tables, chunks):
    (th, tl), (ih, il), _ = tables
    return pl.pallas_call(
        forward_body,
        in_specs=[SMEM_SPEC, HBM_SPEC, VMEM_SPEC] + [HBM_SPEC] * 4 + [VMEM_SPEC] * 7,
        out_specs=(VMEM_SPEC, HBM_SPEC),
        scratch_shapes=[
            pltpu.VMEM((NF, 2, 2, SB, LANE), bf16),
            pltpu.VMEM((2, 2 * NF, NT), bf16),
            pltpu.VMEM((2, NT, 2 * NF), bf16),
            pltpu.VMEM((8, R, R, NT), f32),
            SPEC_ROWS,
            SPEC_ROWS,
            pltpu.SemaphoreType.DMA((3,)),
            pltpu.SemaphoreType.DMA((2,)),
            pltpu.SemaphoreType.DMA((2,)),
        ],
        out_shape=(jax.ShapeDtypeStruct((NT, R * S), f32), pltpu.HBM((NF, 2, 2, S, LANE), bf16)),
        compiler_params=pltpu.CompilerParams(vmem_limit_bytes=24 << 20),
        name="forward",
    )(row, *in_hbm([k1]), in_vmem(k2), *in_hbm([th, tl, ih, il]), *chunks)


def adjoint_body(core_ref, k_hbm, th_ref, tl_ref, ih_ref, il_ref, *refs):
    nw_ref, own_ref, other_ref, o_ref, k_ref, t_ref, i_ref, w_ref, g_ref, wt_ref, sem, t_sem, i_sem = refs
    t_copies = fetch_tables((th_ref, tl_ref), t_ref, t_sem)
    copies = fetch_blocks(k_hbm, k_ref, sem)
    half = NT // 2
    core = core_ref[0]
    wt_ref[pl.ds(pl.multiple_of(core * half, half), half), :] = own_ref[...]
    wt_ref[pl.ds(pl.multiple_of((1 - core) * half, half), half), :] = other_ref[...]
    for c in t_copies:
        c.wait()
    start(copies[0])
    start(copies[1])
    i_copies = fetch_tables((ih_ref, il_ref), i_ref, i_sem)
    table = (t_ref[0], t_ref[1])
    nw = nw_ref[...]
    low_t = lax.broadcasted_iota(jnp.int32, (NT, LANE), 1) < S
    low_f = lax.broadcasted_iota(jnp.int32, (NF, LANE), 1) < S
    for j in range(R // 2):
        a = wt_ref[:, j * LANE : (j + 1) * LANE] * nw
        b = pltpu.roll(a, S, 1)
        x = jnp.concatenate([jnp.where(low_t, a, b), jnp.where(low_t, b, a)], 1)
        y_re, y_im = transform(table, x[:half], x[half:], 0)
        for n in range(2):
            re = y_re[:, n * LANE : (n + 1) * LANE]
            im = y_im[:, n * LANE : (n + 1) * LANE]
            put_rows(w_ref, 0, 2 * j + n, jnp.where(low_f, re, im))
            put_rows(w_ref, 1, 2 * j + n, jnp.where(low_f, im, -re))
        if j in (3,):
            start(copies[2])

    def body(pair, carry):
        zero = jnp.zeros((4 * R, LANE), bf16)
        lhs, rhs = [], []
        for n in range(2):
            f = 2 * pair + n
            parts = split(jnp.concatenate([get_freq(w_ref, part, f) for part in range(2)], 0))
            own = jnp.concatenate(parts, 0)
            lhs.append(jnp.concatenate([own, zero] if n == 0 else [zero, own], 1))
            for c in range(2):
                rhs.append(jnp.concatenate([k_ref[f, c, 0], k_ref[f, c, 1]], 1))
        out = mm(jnp.concatenate(lhs, 0), jnp.concatenate(rhs, 0), NND)
        for n in range(2):
            own = out[4 * R * n : 4 * R * (n + 1)]
            own = own[: 2 * R] + own[2 * R :]
            put_freq(g_ref, 2 * pair + n, own[:, :LANE] + own[:, LANE:])
        return carry

    for_each_frequency(copies, body)

    for c in i_copies:
        c.wait()
    table = (i_ref[0], i_ref[1])
    for r in range(R):
        spec = jnp.concatenate([get_rows(g_ref, part, r) for part in range(2)], 0)
        y = mm3(split(spec), table, TND)
        o_ref[:, r] = y.reshape(8, R, NT)


def adjoint(core, k_hat, tables, noise, own, other):
    (th, tl), _, (ih, il) = tables
    return pl.pallas_call(
        adjoint_body,
        in_specs=[SMEM_SPEC] + [HBM_SPEC] * 5 + [VMEM_SPEC] * 3,
        out_specs=VMEM_SPEC,
        scratch_shapes=[
            K_SCRATCH,
            pltpu.VMEM((2, 2 * NF, NT), bf16),
            pltpu.VMEM((2, 2 * NF, NT), bf16),
            SPEC_ROWS,
            SPEC_ROWS,
            pltpu.VMEM((NT, R * S), f32),
            pltpu.SemaphoreType.DMA((KB,)),
            pltpu.SemaphoreType.DMA((2,)),
            pltpu.SemaphoreType.DMA((2,)),
        ],
        out_shape=jax.ShapeDtypeStruct((8, R, R, NT), f32),
        compiler_params=pltpu.CompilerParams(vmem_limit_bytes=36 << 20),
        name="adjoint",
    )(core, *in_hbm([k_hat, th, tl, ih, il]), noise, own, other)


Z_STEPS = (1, 3, 2)
X_SWAP = [(i, i ^ 4) for i in range(8)]


def z_shift(d):
    return [(i, (i & 4) | ((i + d) & 3)) for i in range(8)]


CORE_SWAP = [(i, i ^ 1) for i in range(16)]
CHIP_GROUPS = [list(range(0, 16, 2)), list(range(1, 16, 2))]


def local(kernel, history, noise_weight, prior_weight):
    tables = dft_tables()
    row = lax.axis_index("row")
    col = lax.axis_index("col")
    core = col & 1

    by_vector = jnp.swapaxes(history, 0, 1)
    own, other = by_vector[: R // 2], by_vector[R // 2 :]
    across = lax.ppermute(own, "row", X_SWAP)
    along = [lax.ppermute(other, "row", z_shift(d)) for d in Z_STEPS]
    k1 = kernel_dft(kernel, tables[0], 0, 1)
    kernel, k1, across, along = lax.optimization_barrier((kernel, k1, across, along))
    along = jnp.stack([other] + along)
    pair = jnp.stack([own, across])
    own_z = [lax.ppermute(pair, "row", z_shift(d)) for d in Z_STEPS]
    both = lax.ppermute(along, "row", X_SWAP)
    k2 = kernel_dft(kernel, tables[0], 1, S // SB - 1)
    chunks = [own, across, *own_z, along, both]
    by_time = noise_weight.T
    by_time = jnp.concatenate([by_time[: NT // 2], by_time[NT // 2 :][::-1]], 0)
    noise = jnp.concatenate([by_time, by_time], 1)

    data, k_hat = forward(row.reshape(1).astype(jnp.int32), k1, k2, tables, chunks)

    half = NT // 2
    mine = lax.dynamic_slice(data, (core * half, 0), (half, R * S))
    theirs = lax.dynamic_slice(data, ((1 - core) * half, 0), (half, R * S))
    mine = mine + lax.ppermute(theirs, "col", CORE_SWAP)
    parts = lax.all_to_all(
        mine.reshape(8, half // 8, R * S), "col", 0, 0, axis_index_groups=CHIP_GROUPS, tiled=True
    )
    total = parts.sum(0)
    spread = jnp.broadcast_to(total, (8, half // 8, R * S))
    own = lax.all_to_all(spread, "col", 0, 0, axis_index_groups=CHIP_GROUPS, tiled=True).reshape(half, R * S)
    other = lax.ppermute(own, "col", CORE_SWAP)

    grad = adjoint(core.reshape(1).astype(jnp.int32), k_hat, tables, noise, own, other)
    grad = lax.all_to_all(grad, "row", 0, 0, tiled=True).sum(0)
    return jnp.swapaxes(grad, 0, 1) + prior_weight[:, None, None] * history


def solution(mesh):
    in_specs = (
        P("row", "col", None),
        P(("col", "row"), None, None),
        P("row", None),
        P(("col", "row")),
    )
    out_specs = P(("col", "row"), None, None)
    return jax.shard_map(local, mesh=mesh, in_specs=in_specs, out_specs=out_specs, check_vma=False)
```

```python
import math

import jax
import jax.numpy as jnp
import numpy as np
from jax import lax
from jax.experimental import pallas as pl
from jax.experimental.pallas import tpu as pltpu
from jax.sharding import PartitionSpec as P

bf16 = jnp.bfloat16
f32 = jnp.float32
NT = 256
NF = 256
S = 64
PL = 128
R = 16
LANE = 128


def split_np(table):
    high = table.astype(np.float32).astype(np.dtype(bf16))
    low = (table - high.astype(np.float64)).astype(np.float32).astype(np.dtype(bf16))
    return high, low


def dft_tables():
    omega = 2.0 * math.pi * (FREQ_ORDER + 0.5)[:, None] / (2 * NT)

    def folded(times):
        tables = []
        phase = omega * ((NT - 1) / 2 - times)[None, :]
        for table in (np.cos(phase), np.sin(phase)):
            high, low = split_np(table)
            tables.append(np.concatenate([high, low], 0))
        return tables

    after = omega[: NF // 2] * (TIME_ORDER - (NT - 1))[None, :]
    inverse = np.concatenate([np.cos(after), -np.sin(after)], 0) / NF
    after = omega * np.arange(NT)[None, :]
    adjoint_inverse = np.concatenate([np.cos(after), -np.sin(after)], 0) / NF
    return (
        folded(np.arange(NT // 2)),
        split_np(inverse.T.copy()),
        folded(TIME_ORDER[: NT // 2]),
        split_np(adjoint_inverse),
    )


def split(x):
    high = x.astype(bf16)
    return high, (x - high.astype(f32)).astype(bf16)


def in_hbm(arrays):
    return [pltpu.with_memory_space_constraint(jnp.asarray(x), pltpu.HBM) for x in arrays]


def mm(a, b, dims):
    return lax.dot_general(a, b, (dims, ((), ())), preferred_element_type=f32)


NTD = ((1,), (1,))
NND = ((1,), (0,))
TND = ((0,), (0,))


def mm3(a, b, dims):
    return mm(a[0], b[0], dims) + mm(a[0], b[1], dims) + mm(a[1], b[0], dims)


def transform(tables, first, mirrored, axis):
    parts = []
    for table, folded in zip(tables, (first + mirrored, first - mirrored)):
        both = jnp.concatenate([table, table], 1)
        y = mm(both, jnp.concatenate(split(folded), axis), NTD if axis else NND)
        parts.append(y[:NF] + y[NF:])
    return parts


def transform_rows(tables, x):
    half = NT // 2
    back = half - 1 - lax.broadcasted_iota(jnp.int32, (x.shape[0], half), 1)
    return transform(tables, x[:, :half], jnp.take_along_axis(x[:, half:], back, axis=1), 1)


def const_spec(shape):
    return pl.BlockSpec(shape, lambda *_: (0,) * len(shape), pipeline_mode=pl.Buffered(1))


SB = 16
FREQ_ORDER = np.concatenate([np.arange(NF // 2), np.arange(NF - 1, NF // 2 - 1, -1)])
TIME_ORDER = np.concatenate([np.arange(0, NT, 2), np.arange(NT - 1, 0, -2)])
G8 = 8


def kernel_dft_body(x_ref, th_ref, tl_ref, o_ref, sc_ref):
    table = (th_ref[...], tl_ref[...])
    for j in range(0, SB, 2):
        x = x_ref[j : j + 2].reshape(2 * PL, NT)
        for part, y in enumerate(transform_rows(table, x)):
            for q in (j, j + 1):
                group = (q // G8 * 2 + part) * NF * G8
                sc_ref[pl.ds(group + q % G8, NF, stride=G8), :] = y[:, (q - j) * LANE : (q - j + 1) * LANE]
    step = 16
    for c in range(2):

        def body(i, carry):
            base = pl.multiple_of(i * step, step)
            v = jnp.concatenate(
                [
                    sc_ref[
                        pl.ds(pl.multiple_of(((g * 2 + c) * NF + base) * G8, step * G8), step * G8), :
                    ].reshape(step, G8, LANE)
                    for g in range(SB // G8)
                ],
                1,
            )
            high, low = split(v)
            rows = pl.ds(pl.multiple_of(pl.program_id(0) * SB, SB), SB)
            o_ref[pl.ds(base, step), c, 0, rows] = high
            o_ref[pl.ds(base, step), c, 1, rows] = low
            return carry

        lax.fori_loop(0, NF // step, body, 0)


def in_vmem(x):
    return pltpu.with_memory_space_constraint(x, pltpu.VMEM)


def kernel_dft(kernel, tables, first, steps):
    return pl.pallas_call(
        kernel_dft_body,
        grid=(steps,),
        in_specs=[
            pl.BlockSpec((SB, PL, NT), lambda i: (i + first, 0, 0)),
            const_spec((2 * NF, NT // 2)),
            const_spec((2 * NF, NT // 2)),
        ],
        out_specs=pl.BlockSpec(memory_space=pltpu.VMEM),
        out_shape=pltpu.VMEM((NF, 2, 2, steps * SB, LANE), bf16),
        scratch_shapes=[pltpu.VMEM((2 * NF * SB, LANE), f32)],
        compiler_params=pltpu.CompilerParams(vmem_limit_bytes=16 << 20),
        name="kernel_dft",
    )(*in_hbm([kernel, *tables]))


def put_rows(ref, part, q, value):
    group = (part * (R // G8) + q // G8) * NF * G8
    ref[pl.ds(group + q % G8, NF, stride=G8), :] = value


def get_rows(ref, part, q):
    group = (part * (R // G8) + q // G8) * NF * G8
    return ref[pl.ds(group + q % G8, NF, stride=G8), :]


def freq_at(part, g, f):
    return pl.ds(pl.multiple_of(((part * (R // G8) + g) * NF + f) * G8, G8), G8)


def get_freq(ref, part, f):
    return jnp.concatenate([ref[freq_at(part, g, f), :] for g in range(R // G8)], 0)


def put_freq(ref, f, value):
    for part in range(2):
        for g in range(R // G8):
            at = part * R + g * G8
            ref[freq_at(part, g, f), :] = value[at : at + G8]


AHEAD = 3
KB = 8
FB = NF // KB


def fetch_blocks(k_hbm, k_ref, sem):
    return [
        [pltpu.make_async_copy(k_hbm.at[pl.ds(b * FB, FB)], k_ref.at[pl.ds(b * FB, FB)], sem.at[b])]
        for b in range(KB)
    ]


def start(copies):
    for c in copies:
        c.start()


def wait(copies):
    for c in copies:
        c.wait()


def fetch_tables(tables, t_ref, sem):
    copies = [pltpu.make_async_copy(table, t_ref.at[n], sem.at[n]) for n, table in enumerate(tables)]
    for c in copies:
        c.start()
    return copies


def for_each_frequency(copies, body):
    for b in range(KB):
        wait(copies[b])
        if b + AHEAD < KB:
            start(copies[b + AHEAD])
        lax.fori_loop(b * FB // 2, (b + 1) * FB // 2, body, 0, unroll=16)


def forward_body(row_ref, k1_hbm, k2_ref, th_ref, tl_ref, ih_ref, il_ref, *refs):
    own, across, *own_z = refs[:5]
    along, both = refs[5:7]
    o_ref, k_hbm, k1_ref, t_ref, i_ref, hist_ref, h_ref, d_ref, sem, t_sem, i_sem = refs[7:]
    t_copies = fetch_tables((th_ref, tl_ref), t_ref, t_sem)
    k1_copy = pltpu.make_async_copy(k1_hbm, k1_ref, sem.at[0])
    k1_out = pltpu.make_async_copy(k1_ref, k_hbm.at[:, :, :, pl.ds(0, SB)], sem.at[1])
    k2_out = pltpu.make_async_copy(k2_ref, k_hbm.at[:, :, :, pl.ds(SB, S - SB)], sem.at[2])
    hi, z = row_ref[0] >> 2, row_ref[0] & 3
    for n, d in enumerate((0,) + Z_STEPS):
        for m in range(2):
            at = (hi if m == 0 else 1 - hi) * 4 + ((z - d) & 3)
            first = (own, across)[m][...] if n == 0 else own_z[n - 1][m]
            hist_ref[at, : R // 2] = first
            hist_ref[at, R // 2 :] = (along, both)[m][n]
    for c in t_copies:
        c.wait()
    k1_copy.start()
    i_copies = fetch_tables((ih_ref, il_ref), i_ref, i_sem)
    table = (t_ref[0], t_ref[1])
    for r in range(0, R, 2):
        x = jnp.concatenate([hist_ref[:, q].reshape(PL, NT) for q in (r, r + 1)], 0)
        for part, y in enumerate(transform_rows(table, x)):
            for q in (r, r + 1):
                put_rows(h_ref, part, q, y[:, (q - r) * LANE : (q - r + 1) * LANE])

    def body(pair, carry):
        lhs, rhs = [], []
        for f in (2 * pair, 2 * pair + 1):
            re = split(get_freq(h_ref, 0, f))
            im = split(get_freq(h_ref, 1, f))
            for n in range(2):
                lhs.append(jnp.concatenate([re[n], -im[n]], 1))
                lhs.append(jnp.concatenate([im[n], re[n]], 1))
            rhs.append(
                jnp.concatenate(
                    [
                        jnp.concatenate([k[f, c, n] for n in range(2) for k in (k1_ref, k2_ref)], 0)
                        for c in range(2)
                    ],
                    1,
                )
            )
        out = mm(jnp.concatenate(lhs, 0), jnp.concatenate(rhs, 0), NTD)
        for n in range(2):
            own = out[4 * R * n : 4 * R * (n + 1), LANE * n : LANE * (n + 1)]
            put_freq(d_ref, 2 * pair + n, own[: 2 * R] + own[2 * R :])
        return carry

    k1_copy.wait()
    k1_out.start()
    k2_out.start()
    lax.fori_loop(0, NF // 2, body, 0, unroll=16)

    for c in i_copies:
        c.wait()
    table_even = (i_ref[0, : NT // 2], i_ref[1, : NT // 2])
    table_odd = (i_ref[0, NT // 2 :], i_ref[1, NT // 2 :])
    lane = lax.broadcasted_iota(jnp.int32, (NT, LANE), 1)
    for r in range(0, R, 2):
        re, im = [jnp.concatenate([get_rows(d_ref, part, q) for q in (r, r + 1)], 1) for part in range(2)]
        re, re_mirror = re[: NF // 2], re[NF // 2 :]
        im, im_mirror = im[: NF // 2], im[NF // 2 :]
        even = split(jnp.concatenate([re - re_mirror, im + im_mirror], 0))
        odd = split(jnp.concatenate([re + re_mirror, im - im_mirror], 0))
        y = jnp.concatenate([mm3(table_even, even, NND), mm3(table_odd, odd, NND)], 0)
        halves = [y[:, :LANE] + pltpu.roll(y[:, :LANE], S, 1), y[:, LANE:] + pltpu.roll(y[:, LANE:], S, 1)]
        o_ref[:, (r // 2) * LANE : (r // 2 + 1) * LANE] = jnp.where(lane < S, halves[0], halves[1])
    k1_out.wait()
    k2_out.wait()


VMEM_SPEC = pl.BlockSpec(memory_space=pltpu.VMEM)
HBM_SPEC = pl.BlockSpec(memory_space=pl.ANY)
SMEM_SPEC = pl.BlockSpec(memory_space=pltpu.SMEM)
SPEC_ROWS = pltpu.VMEM((2 * NF * R, LANE), f32)
K_SCRATCH = pltpu.VMEM((NF, 2, 2, S, LANE), bf16)


def forward(row, k1, k2, tables, chunks):
    (th, tl), (ih, il) = tables[:2]
    return pl.pallas_call(
        forward_body,
        in_specs=[SMEM_SPEC, HBM_SPEC, VMEM_SPEC] + [HBM_SPEC] * 4 + [VMEM_SPEC] * 7,
        out_specs=(VMEM_SPEC, HBM_SPEC),
        scratch_shapes=[
            pltpu.VMEM((NF, 2, 2, SB, LANE), bf16),
            pltpu.VMEM((2, 2 * NF, NT // 2), bf16),
            pltpu.VMEM((2, NT, NF), bf16),
            pltpu.VMEM((8, R, R, NT), f32),
            SPEC_ROWS,
            SPEC_ROWS,
            pltpu.SemaphoreType.DMA((3,)),
            pltpu.SemaphoreType.DMA((2,)),
            pltpu.SemaphoreType.DMA((2,)),
        ],
        out_shape=(jax.ShapeDtypeStruct((NT, R * S), f32), pltpu.HBM((NF, 2, 2, S, LANE), bf16)),
        compiler_params=pltpu.CompilerParams(vmem_limit_bytes=24 << 20),
        name="forward",
    )(row, *in_hbm([k1]), in_vmem(k2), *in_hbm([th, tl, ih, il]), *chunks)


def adjoint_body(core_ref, row_ref, k_hbm, th_ref, tl_ref, ih_ref, il_ref, *refs):
    nw_ref, own_ref, other_ref = refs[:3]
    along_refs, across_refs = refs[3:7], refs[7:9]
    k_ref, t_ref, i_ref, w_ref, g_ref, wt_ref, y_ref, sem, t_sem, i_sem = refs[9:]
    t_copies = fetch_tables((th_ref, tl_ref), t_ref, t_sem)
    copies = fetch_blocks(k_hbm, k_ref, sem)
    half = NT // 2
    core = core_ref[0]
    wt_ref[pl.ds(pl.multiple_of(core * half, half), half), :] = own_ref[...]
    wt_ref[pl.ds(pl.multiple_of((1 - core) * half, half), half), :] = other_ref[...]
    for c in t_copies:
        c.wait()
    start(copies[0])
    start(copies[1])
    i_copies = fetch_tables((ih_ref, il_ref), i_ref, i_sem)
    table = (t_ref[0], t_ref[1])
    nw = nw_ref[...]
    low_t = lax.broadcasted_iota(jnp.int32, (NT, LANE), 1) < S
    low_f = lax.broadcasted_iota(jnp.int32, (NF, LANE), 1) < S
    for j in range(R // 2):
        a = wt_ref[:, j * LANE : (j + 1) * LANE] * nw
        b = pltpu.roll(a, S, 1)
        x = jnp.concatenate([jnp.where(low_t, a, b), jnp.where(low_t, b, a)], 1)
        y_re, y_im = transform(table, x[:half], x[half:], 0)
        for n in range(2):
            re = y_re[:, n * LANE : (n + 1) * LANE]
            im = y_im[:, n * LANE : (n + 1) * LANE]
            put_rows(w_ref, 0, 2 * j + n, jnp.where(low_f, re, im))
            put_rows(w_ref, 1, 2 * j + n, jnp.where(low_f, im, -re))
        if j in (3,):
            start(copies[2])

    def body(pair, carry):
        zero = jnp.zeros((4 * R, LANE), bf16)
        lhs, rhs = [], []
        for n in range(2):
            f = 2 * pair + n
            parts = split(jnp.concatenate([get_freq(w_ref, part, f) for part in range(2)], 0))
            own = jnp.concatenate(parts, 0)
            lhs.append(jnp.concatenate([own, zero] if n == 0 else [zero, own], 1))
            for c in range(2):
                rhs.append(jnp.concatenate([k_ref[f, c, 0], k_ref[f, c, 1]], 1))
        out = mm(jnp.concatenate(lhs, 0), jnp.concatenate(rhs, 0), NND)
        for n in range(2):
            own = out[4 * R * n : 4 * R * (n + 1)]
            own = own[: 2 * R] + own[2 * R :]
            put_freq(g_ref, 2 * pair + n, own[:, :LANE] + own[:, LANE:])
        return carry

    for_each_frequency(copies, body)

    for c in i_copies:
        c.wait()
    table = (i_ref[0], i_ref[1])
    for r in range(R):
        spec = jnp.concatenate([get_rows(g_ref, part, r) for part in range(2)], 0)
        y = mm3(split(spec), table, TND)
        y_ref[r] = y
    hi, z = row_ref[0] >> 2, row_ref[0] & 3
    for n, d in enumerate((0,) + Z_STEPS):
        for m in range(2):
            to = (hi if m == 0 else 1 - hi) * 4 + ((z + d) & 3)
            piece = pl.ds(pl.multiple_of(to * R, R), R)
            along_refs[n][m] = y_ref[: R // 2, piece]
            across_refs[m][n] = y_ref[R // 2 :, piece]


def adjoint(core, row, k_hat, tables, noise, own, other):
    (th, tl), (ih, il) = tables[2:]
    return pl.pallas_call(
        adjoint_body,
        in_specs=[SMEM_SPEC] * 2 + [HBM_SPEC] * 5 + [VMEM_SPEC] * 3,
        out_specs=(VMEM_SPEC,) * 6,
        scratch_shapes=[
            K_SCRATCH,
            pltpu.VMEM((2, 2 * NF, NT // 2), bf16),
            pltpu.VMEM((2, 2 * NF, NT), bf16),
            SPEC_ROWS,
            SPEC_ROWS,
            pltpu.VMEM((NT, R * S), f32),
            pltpu.VMEM((R, PL, NT), f32),
            pltpu.SemaphoreType.DMA((KB,)),
            pltpu.SemaphoreType.DMA((2,)),
            pltpu.SemaphoreType.DMA((2,)),
        ],
        out_shape=(jax.ShapeDtypeStruct((2, R // 2, R, NT), f32),) * 4
        + (jax.ShapeDtypeStruct((4, R // 2, R, NT), f32),) * 2,
        compiler_params=pltpu.CompilerParams(vmem_limit_bytes=36 << 20),
        name="adjoint",
    )(core, row, *in_hbm([k_hat, th, tl, ih, il]), noise, own, other)


Z_STEPS = (1, 3, 2)
X_SWAP = [(i, i ^ 4) for i in range(8)]


def z_shift(d):
    return [(i, (i & 4) | ((i + d) & 3)) for i in range(8)]


CORE_SWAP = [(i, i ^ 1) for i in range(16)]
CHIP_GROUPS = [list(range(0, 16, 2)), list(range(1, 16, 2))]


def local(kernel, history, noise_weight, prior_weight):
    tables = dft_tables()
    row = lax.axis_index("row")
    col = lax.axis_index("col")
    core = col & 1

    by_vector = jnp.swapaxes(history, 0, 1)
    own, other = by_vector[: R // 2], by_vector[R // 2 :]
    across = lax.ppermute(own, "row", X_SWAP)
    along = [lax.ppermute(other, "row", z_shift(d)) for d in Z_STEPS]
    k1 = kernel_dft(kernel, tables[0], 0, 1)
    kernel, k1, across, along = lax.optimization_barrier((kernel, k1, across, along))
    along = jnp.stack([other] + along)
    pair = jnp.stack([own, across])
    own_z = [lax.ppermute(pair, "row", z_shift(d)) for d in Z_STEPS]
    both = lax.ppermute(along, "row", X_SWAP)
    k2 = kernel_dft(kernel, tables[0], 1, S // SB - 1)
    chunks = [own, across, *own_z, along, both]
    by_time = noise_weight.T
    by_time = jnp.concatenate([by_time[::2], by_time[1::2][::-1]], 0)
    noise = jnp.concatenate([by_time, by_time], 1)

    data, k_hat = forward(row.reshape(1).astype(jnp.int32), k1, k2, tables, chunks)

    half = NT // 2
    mine = lax.dynamic_slice(data, (core * half, 0), (half, R * S))
    theirs = lax.dynamic_slice(data, ((1 - core) * half, 0), (half, R * S))
    mine = mine + lax.ppermute(theirs, "col", CORE_SWAP)
    parts = lax.all_to_all(
        mine.reshape(8, half // 8, R * S), "col", 0, 0, axis_index_groups=CHIP_GROUPS, tiled=True
    )
    total = parts.sum(0)
    spread = jnp.broadcast_to(total, (8, half // 8, R * S))
    own = lax.all_to_all(spread, "col", 0, 0, axis_index_groups=CHIP_GROUPS, tiled=True).reshape(half, R * S)
    other = lax.ppermute(own, "col", CORE_SWAP)

    row = row.reshape(1).astype(jnp.int32)
    *to_z, to_own, to_across = adjoint(core.reshape(1).astype(jnp.int32), row, k_hat, tables, noise, own, other)
    from_across = lax.ppermute(to_across, "row", X_SWAP)
    from_z = [lax.ppermute(part, "row", z_shift(d)) for part, d in zip(to_z[1:], Z_STEPS)]
    second = [to_own[n] + from_across[n] for n in range(4)]
    first = [to_z[0][m] + from_z[0][m] + from_z[1][m] + from_z[2][m] for m in range(2)]
    second_z = [lax.ppermute(part, "row", z_shift(d)) for part, d in zip(second[1:], Z_STEPS)]
    first_across = lax.ppermute(first[1], "row", X_SWAP)
    grad = jnp.concatenate([first[0] + first_across, second[0] + second_z[0] + second_z[1] + second_z[2]], 0)
    return jnp.swapaxes(grad, 0, 1) + prior_weight[:, None, None] * history


def solution(mesh):
    in_specs = (
        P("row", "col", None),
        P(("col", "row"), None, None),
        P("row", None),
        P(("col", "row")),
    )
    out_specs = P(("col", "row"), None, None)
    return jax.shard_map(local, mesh=mesh, in_specs=in_specs, out_specs=out_specs, check_vma=False)
```
